128 devices in a mesh: node: 16 (over z, y), local: 8 (over x, core).
Axes of the slice: x: 4, y: 4, z: 4, core: 2. Of those that a mesh axis runs over, the one named last changes fastest.
Arguments:
- tokens: bfloat16 [16384, 3584], P(('node', 'local')), may hold values from -6 to 6
- expert_ids: int32 [16384, 8], P(('node', 'local')), may hold values from 0 to 127, as said below
- gate_quanta: int32 [16384, 8], P(('node', 'local')), may hold values from 1 to 65535
- w_gate: bfloat16 [128, 3584, 1024], P(('node', 'local')), may hold values from -0.09375 to 0.09375
- w_up: bfloat16 [128, 3584, 1024], P(('node', 'local')), may hold values from -0.09375 to 0.09375
- w_down: bfloat16 [128, 1024, 3584], P(('node', 'local')), may hold values from -0.1875 to 0.1875
Outputs:
- mixed_rows: bfloat16 [16384, 3584], P(('node', 'local'))
The draws below stay inside these ranges and needn't reach their ends.
Inputs may be any that keep to these rules, and one draw needn't show every extreme that they name: `expert_ids`: each row names 8 different experts that lie in at most 4 node groups, experts g * 8 to (g + 1) * 8 - 1 forming group g; in the rows of one device no expert is named more than 10 times and no node group is chosen by more than 32 tokens.
All inputs are finite; a program needn't handle non-finite values.
Results may differ from the reference program's by a relative error of at most 0.0058.
Values may be sent and summed in bfloat16 or wider, within the bound.
No kernel may reach another device: no remote copies, remote signals or barrier semaphores. Data moves between devices by JAX's collectives and lax.ppermute only.
A program may use at most 192 MiB of HBM per device.

```python
import jax
import jax.numpy as jnp
from jax import lax

D = 3584
HID = 1024
TOPK = 8
NODE_LIMIT = 4
TOK_DEV = 128
TOKENS = 16384
EXPERTS = 128
NODE_GROUPS = 16
GROUP_SIZE = 8
MOST = 10
GROUP_MOST = 32
CAP = 1152


def shuffle_row(row_key, row_values):
    return jax.random.permutation(row_key, row_values)


def draw_expert_ids(key, part):
    blocks = TOKENS // TOK_DEV
    per_group = GROUP_MOST
    stride = TOK_DEV // NODE_GROUPS
    mean_load = TOK_DEV * TOPK // EXPERTS
    lowest = 2 * mean_load - MOST
    loads = jnp.full((GROUP_SIZE,), mean_load, jnp.int32)
    loads = loads.at[0].set(MOST).at[1].set(MOST).at[2].set(lowest).at[3].set(lowest)
    bounds = jnp.cumsum(loads)
    ticket_spots = jnp.arange(2 * per_group, dtype=jnp.int32)
    ticket = jnp.sum((ticket_spots[:, None] >= bounds[None, :]).astype(jnp.int32), axis=1)
    hot_local = jax.random.randint(jax.random.fold_in(key, 11), (NODE_GROUPS,), 0, GROUP_SIZE).astype(jnp.int32)
    spots = jnp.arange(GROUP_SIZE, dtype=jnp.int32)

    def order_one(order_key, hot):
        perm_key = jax.random.fold_in(order_key, 1)
        coin_key = jax.random.fold_in(order_key, 2)
        perm = jax.random.permutation(perm_key, GROUP_SIZE).astype(jnp.int32)
        coin = jax.random.randint(coin_key, (), 0, 4)
        target = jnp.where(coin < 3, 0, 2).astype(jnp.int32)
        where_hot = jnp.sum(jnp.where(perm == hot, spots, 0)).astype(jnp.int32)
        displaced = jnp.sum(jnp.where(spots == target, perm, 0)).astype(jnp.int32)
        perm = jnp.where(spots == where_hot, displaced, perm)
        perm = jnp.where(spots == target, hot, perm)
        return perm.astype(jnp.int32)

    def pick_permute(pick_key):
        return jax.random.permutation(pick_key, per_group)

    def one_block(block_key):
        label_key = jax.random.fold_in(block_key, 1)
        group_key = jax.random.fold_in(block_key, 2)
        pick_key = jax.random.fold_in(block_key, 3)
        column_key = jax.random.fold_in(block_key, 4)
        order_key = jax.random.fold_in(block_key, 5)
        local_order = jax.vmap(order_one)(jax.random.split(order_key, NODE_GROUPS), hot_local)
        labels = jax.random.permutation(label_key, TOK_DEV)
        group_perm = jax.random.permutation(group_key, NODE_GROUPS)
        pick_perm = jax.vmap(pick_permute)(jax.random.split(pick_key, NODE_GROUPS))
        remainder = labels % NODE_GROUPS
        quotient = labels // NODE_GROUPS
        columns = []
        for turn in range(NODE_LIMIT):
            turned = (remainder + turn) % NODE_GROUPS
            picked = turn * stride + quotient
            group = group_perm[turned]
            shuffled = pick_perm[group, picked]
            first_local = local_order[group, ticket[shuffled]]
            second_local = local_order[group, ticket[shuffled + per_group]]
            columns.append(group * GROUP_SIZE + first_local)
            columns.append(group * GROUP_SIZE + second_local)
        chosen = jnp.stack(columns, axis=1).astype(jnp.int32)
        row_keys = jax.random.split(column_key, TOK_DEV)
        return jax.vmap(shuffle_row)(row_keys, chosen)
    block_keys = jax.random.split(jax.random.fold_in(key, 7), blocks)
    return jax.vmap(one_block)(block_keys).reshape(TOKENS, TOPK).astype(jnp.int32)


def plant(result, own_key, least, high):
    longest = result.shape.index(max(result.shape))
    spots = []
    for shift in (0, 1):
        where = [jax.random.randint(jax.random.fold_in(own_key, axis), (), 0, length) for axis, length in enumerate(result.shape)]
        where[longest] = (where[longest] + shift) % result.shape[longest]
        spots.append(tuple(where))
    return result.at[spots[0]].set(least).at[spots[1]].set(high)


def block_scale(rng, dims, shards, least, high):
    loudness = 1.0
    for dim, blocks in shards:
        draws = jax.random.uniform(jax.random.fold_in(jax.random.fold_in(rng, 6), dim), (blocks,), jnp.float32, least / len(shards), high / len(shards))
        loudness = loudness * jnp.repeat(jnp.exp(draws), dims[dim] // blocks).reshape((-1,) + (1,) * (len(dims) - 1 - dim))
    return loudness


def scatter_about(key, dims, spread, reach, shards=(), kind=jnp.bfloat16):
    factor_of = block_scale(key, dims, shards, -0.22, 0.18) if shards else 1.0
    values = jax.random.normal(key, dims, jnp.float32) * spread * factor_of
    return jnp.minimum(jnp.maximum(values, -reach), reach).astype(kind)


def setup_inputs(seed: int = 0) -> dict:
    arg_keys = jax.random.split(jax.random.key(seed), 7)
    return {
        "tokens": scatter_about(arg_keys[0], (TOKENS, D), 1.0, 6.0, ((0, 128),)),
        "expert_ids": draw_expert_ids(jax.random.fold_in(arg_keys[6], 71), 0),
        "gate_quanta": plant(jax.random.randint(arg_keys[2], (TOKENS, TOPK), 1, 65536), jax.random.fold_in(arg_keys[2], 1), 1, 65535).astype(jnp.int32),
        "w_gate": scatter_about(arg_keys[3], (EXPERTS, D, HID), D ** -0.5, 0.09375, ((0, 128),)),
        "w_up": scatter_about(arg_keys[4], (EXPERTS, D, HID), D ** -0.5, 0.09375, ((0, 128),)),
        "w_down": scatter_about(arg_keys[5], (EXPERTS, HID, D), HID ** -0.5, 0.1875, ((0, 128),)),
    }


ROUTED_SCALE = 2.5


def reference(tokens, expert_ids, gate_quanta, w_gate, w_up, w_down):
    quanta = gate_quanta.astype(jnp.float32)
    gate_scale = ROUTED_SCALE * quanta / jnp.sum(quanta, axis=1, keepdims=True)
    onehot = (expert_ids[:, :, None] == jnp.arange(EXPERTS, dtype=jnp.int32)[None, None, :]).astype(jnp.int32)
    per_token = jnp.sum(onehot, axis=1)
    earlier_count = jnp.cumsum(per_token, axis=0) - per_token
    position = jnp.sum(onehot * earlier_count[:, None, :], axis=2)
    kept_mask = position < CAP
    dump_slot = EXPERTS * CAP
    slot_index = jnp.where(kept_mask, expert_ids * CAP + position, dump_slot).astype(jnp.int32)
    token_index = jnp.broadcast_to(jnp.arange(TOKENS, dtype=jnp.int32)[:, None], expert_ids.shape)
    source_table = jnp.zeros((dump_slot + 1,), jnp.int32).at[slot_index.reshape(-1)].set(token_index.reshape(-1))
    source_table = source_table[:dump_slot].reshape(EXPERTS, CAP)
    weight_mix = jnp.where(kept_mask, gate_scale, jnp.zeros_like(gate_scale))
    weight_table = jnp.zeros((dump_slot + 1,), jnp.float32).at[slot_index.reshape(-1)].set(weight_mix.reshape(-1))
    weight_table = weight_table[:dump_slot].reshape(EXPERTS, CAP)

    def one_expert(total, inputs):
        table_row, weight_row, gate_w, up_w, down_w = inputs
        chosen = tokens[table_row]
        gate_part = jnp.dot(chosen, gate_w, preferred_element_type=jnp.float32)
        up_part = jnp.dot(chosen, up_w, preferred_element_type=jnp.float32)
        hidden = (jax.nn.silu(gate_part) * up_part).astype(jnp.bfloat16)
        expert_out = jnp.dot(hidden, down_w, preferred_element_type=jnp.float32).astype(jnp.bfloat16)
        total = total.at[table_row].add(weight_row[:, None] * expert_out.astype(jnp.float32))
        return total, None

    start = jnp.zeros((TOKENS, D), jnp.float32)
    mixed_rows, unused = lax.scan(one_expert, start, (source_table, weight_table, w_gate, w_up, w_down))
    return mixed_rows.astype(jnp.bfloat16)
```

```python
import jax
import jax.numpy as jnp
from jax import lax
from jax.experimental import pallas as pl
from jax.experimental.pallas import tpu as pltpu
from jax.sharding import PartitionSpec as P

ROUTED_SCALE = 2.5
SUB = 8
EXTRA = 2
PIECES = 4
LANES = 128
MARK = 1048576.0
VMEM_BYTES = 58 * 1024 * 1024
BF16 = jnp.bfloat16
F32 = jnp.float32


def _iota(shape, dim):
    return lax.broadcasted_iota(jnp.int32, shape, dim)


def _dot(a, b):
    return jnp.dot(a, b, preferred_element_type=F32)


def _chosen(ids_t_ref, experts):
    top, toks = ids_t_ref.shape
    row = _iota((experts, toks), 0)
    total = jnp.zeros((experts, toks), F32)
    for k in range(top):
        total = total + (ids_t_ref[k : k + 1, :] == row).astype(F32)
    return total


def _ranks(chosen):
    toks = chosen.shape[1]
    before = (_iota((toks, toks), 0) < _iota((toks, toks), 1)).astype(BF16)
    return jnp.where(chosen > 0, _dot(chosen.astype(BF16), before), -1.0)


def dispatch_body(ids_t_ref, tokens_ref, out_ref, rank_ref):
    toks, width = tokens_ref.shape
    experts = rank_ref.shape[0]
    rows = out_ref.shape[0]
    piece = width // PIECES

    @pl.when(pl.program_id(0) == 0)
    def _():
        rank_ref[...] = _ranks(_chosen(ids_t_ref, experts)).astype(BF16)

    row = _iota((rows, experts), 0) + pl.program_id(0) * rows
    spread = (row // SUB == _iota((rows, experts), 1)).astype(BF16)
    rank = _dot(spread, rank_ref[...]).astype(jnp.int32)
    sub = _iota((rows, toks), 0) % SUB
    pick = (rank == sub).astype(BF16)
    main = _dot(pick, tokens_ref[...])
    filled = jnp.sum(pick.astype(F32), axis=1, keepdims=True)
    out_ref[:, 0:LANES] = jnp.where(filled > 0, main[:, 0:LANES], MARK).astype(BF16)
    out_ref[:, LANES:width] = main[:, LANES:].astype(BF16)
    extra = rank == SUB + sub // PIECES
    acc = jnp.zeros((rows, piece), F32)
    for c in range(PIECES):
        part = (extra & (sub % PIECES == c)).astype(BF16)
        acc = acc + _dot(part, tokens_ref[:, c * piece : (c + 1) * piece])
    filled = jnp.sum(extra.astype(F32), axis=1, keepdims=True)
    out_ref[:, width : width + LANES] = jnp.where(filled > 0, acc[:, 0:LANES], MARK).astype(BF16)
    out_ref[:, width + LANES :] = acc[:, LANES:].astype(BF16)


def dispatch(ids_t, tokens, experts):
    toks, width = tokens.shape
    rows = 256
    wide = width + width // PIECES
    return pl.pallas_call(
        dispatch_body,
        grid=(experts * SUB // rows,),
        in_specs=[
            pl.BlockSpec(ids_t.shape, lambda i: (0, 0)),
            pl.BlockSpec(tokens.shape, lambda i: (0, 0)),
        ],
        out_specs=pl.BlockSpec((rows, wide), lambda i: (i, 0)),
        out_shape=jax.ShapeDtypeStruct((experts * SUB, wide), BF16),
        scratch_shapes=[pltpu.VMEM((experts, toks), BF16)],
        compiler_params=pltpu.CompilerParams(vmem_limit_bytes=VMEM_BYTES),
        name="dispatch",
    )(ids_t, tokens)


W_CHUNKS = 8


def expert_body(capacity, arrived_ref, gate_hbm, up_hbm, down_hbm, out_ref, gate_w, up_w, down_w, x_ref, g_ref, u_ref, h_ref, seen_ref, sems):
    rows, wide = arrived_ref.shape
    width, hid = gate_w.shape
    piece = width // PIECES
    devs = rows // SUB
    extras = devs * EXTRA
    step = pl.program_id(0)
    kc = width // W_CHUNKS
    hc = hid // 2

    def gate_copy(k):
        s = pl.ds(k * kc, kc)
        return pltpu.make_async_copy(gate_hbm.at[s], gate_w.at[s], sems.at[k])

    def up_copy(k):
        s = pl.ds(k * kc, kc)
        return pltpu.make_async_copy(up_hbm.at[s], up_w.at[s], sems.at[W_CHUNKS + k])

    def down_copy(k):
        s = pl.ds(k * hc, hc)
        return pltpu.make_async_copy(down_hbm.at[s], down_w.at[s], sems.at[2 * W_CHUNKS + k])

    @pl.when(step == 0)
    def _():
        for k in range(W_CHUNKS):
            gate_copy(k).start()
            up_copy(k).start()
        for k in range(2):
            down_copy(k).start()
        seen_ref[...] = jnp.zeros_like(seen_ref)

    src = _iota((rows, rows), 0)
    order = (_iota((rows, rows), 1) == (src % extras) * PIECES + src // extras).astype(BF16)
    extra = _dot(order, arrived_ref[:, width:]).astype(BF16)
    x_ref[0:rows, :] = arrived_ref[:, 0:width]
    for c in range(PIECES):
        x_ref[rows : rows + extras, c * piece : (c + 1) * piece] = extra[c * extras : (c + 1) * extras]

    total = rows + extras
    live = (x_ref[:, 0:LANES].astype(F32) < MARK * 0.5).astype(BF16)
    row = _iota((total, total), 0)
    dev = jnp.where(row < rows, row // SUB, (row - rows) // EXTRA)
    col = _iota((total, total), 1)
    col_dev = jnp.where(col < rows, col // SUB, (col - rows) // EXTRA)
    earlier = _dot((col_dev < dev).astype(BF16), live)
    lane_row = _iota((total, LANES), 0)
    slot = jnp.where(lane_row < rows, lane_row % SUB, SUB + (lane_row - rows) % EXTRA)
    position = seen_ref[0:1, :] + earlier + slot.astype(F32)
    kept = (live.astype(F32) > 0) & (position < capacity)
    seen_ref[0:1, :] = seen_ref[0:1, :] + jnp.sum(live.astype(F32), axis=0, keepdims=True)

    @pl.when(step == 0)
    def _():
        for k in range(W_CHUNKS):
            gate_copy(k).wait()
            up_copy(k).wait()
            x = x_ref[:, k * kc : (k + 1) * kc]
            g = _dot(x, gate_w[k * kc : (k + 1) * kc, :])
            u = _dot(x, up_w[k * kc : (k + 1) * kc, :])
            if k == 0:
                g_ref[...] = g
                u_ref[...] = u
            else:
                g_ref[...] += g
                u_ref[...] += u

    @pl.when(step > 0)
    def _():
        g_ref[...] = _dot(x_ref[...], gate_w[...])
        u_ref[...] = _dot(x_ref[...], up_w[...])

    for j in range(hid // LANES):
        s = slice(j * LANES, (j + 1) * LANES)
        g = g_ref[:, s]
        h_ref[:, s] = jnp.where(kept, g / (1.0 + jnp.exp(-g)) * u_ref[:, s], 0.0).astype(BF16)

    @pl.when(step == 0)
    def _():
        for k in range(2):
            down_copy(k).wait()

    out_ref[:, 0:width] = _dot(h_ref[0:rows, :], down_w[...]).astype(BF16)
    extra_out = _dot(h_ref[rows:, :], down_w[...]).astype(BF16)
    stacked = jnp.concatenate([extra_out[:, c * piece : (c + 1) * piece] for c in range(PIECES)], axis=0)
    dst = _iota((rows, rows), 0)
    back = (_iota((rows, rows), 1) == (dst % PIECES) * extras + dst // PIECES).astype(BF16)
    out_ref[:, width:] = _dot(back, stacked).astype(BF16)


def expert(arrived, w_gate, w_up, w_down, capacity):
    total_rows, wide = arrived.shape
    width, hid = w_gate.shape
    rows = 256
    full = rows + rows // SUB * EXTRA
    block = pl.BlockSpec((rows, wide), lambda i: (i, 0))
    anywhere = pl.BlockSpec(memory_space=pl.ANY)

    def body(*refs):
        expert_body(float(capacity), *refs)

    return pl.pallas_call(
        body,
        grid=(total_rows // rows,),
        in_specs=[block, anywhere, anywhere, anywhere],
        out_specs=block,
        out_shape=jax.ShapeDtypeStruct(arrived.shape, BF16),
        scratch_shapes=[
            pltpu.VMEM((width, hid), BF16),
            pltpu.VMEM((width, hid), BF16),
            pltpu.VMEM((hid, width), BF16),
            pltpu.VMEM((full, width), BF16),
            pltpu.VMEM((full, hid), F32),
            pltpu.VMEM((full, hid), F32),
            pltpu.VMEM((full, hid), BF16),
            pltpu.VMEM((8, LANES), F32),
            pltpu.SemaphoreType.DMA((2 * W_CHUNKS + 2,)),
        ],
        compiler_params=pltpu.CompilerParams(vmem_limit_bytes=VMEM_BYTES),
        name="expert",
    )(arrived, w_gate, w_up, w_down)


def combine_body(ids_t_ref, quanta_t_ref, back_ref, out_ref, rank_ref, gate_ref, acc_ref):
    toks, width = out_ref.shape
    rows = back_ref.shape[0]
    experts = rank_ref.shape[1]
    piece = width // PIECES
    step = pl.program_id(0)

    @pl.when(step == 0)
    def _():
        rank_ref[...] = _ranks(_chosen(ids_t_ref, experts)).T.astype(BF16)
        quanta = quanta_t_ref[...].astype(F32)
        scale = ROUTED_SCALE * quanta / jnp.sum(quanta, axis=0, keepdims=True)
        row = _iota((experts, toks), 0)
        gate = jnp.zeros((experts, toks), F32)
        for k in range(ids_t_ref.shape[0]):
            gate = gate + jnp.where(ids_t_ref[k : k + 1, :] == row, scale[k : k + 1, :], 0.0)
        gate = gate.T
        high = gate.astype(BF16)
        gate_ref[0:toks, :] = high
        gate_ref[toks:, :] = (gate - high.astype(F32)).astype(BF16)
        acc_ref[...] = jnp.zeros_like(acc_ref)

    col = _iota((experts, rows), 1) + step * rows
    spread = (col // SUB == _iota((experts, rows), 0)).astype(BF16)
    rank = _dot(rank_ref[...], spread).astype(jnp.int32)
    gate = _dot(gate_ref[...], spread)
    rank = jnp.concatenate([rank, rank], axis=0)
    sub = _iota((2 * toks, rows), 1) % SUB
    acc_ref[...] += _dot(jnp.where(rank == sub, gate, 0.0).astype(BF16), back_ref[:, 0:width])
    extra = jnp.where(rank == SUB + sub // PIECES, gate, 0.0)
    for c in range(PIECES):
        part = jnp.where(sub % PIECES == c, extra, 0.0).astype(BF16)
        acc_ref[:, c * piece : (c + 1) * piece] += _dot(part, back_ref[:, width:])

    @pl.when(step == pl.num_programs(0) - 1)
    def _():
        out_ref[...] = (acc_ref[0:toks, :] + acc_ref[toks:, :]).astype(BF16)


def combine(ids_t, quanta_t, back, experts):
    top, toks = ids_t.shape
    total_rows, wide = back.shape
    width = wide * PIECES // (PIECES + 1)
    rows = 256
    small = pl.BlockSpec((top, toks), lambda i: (0, 0))
    return pl.pallas_call(
        combine_body,
        grid=(total_rows // rows,),
        in_specs=[small, small, pl.BlockSpec((rows, wide), lambda i: (i, 0))],
        out_specs=pl.BlockSpec((toks, width), lambda i: (0, 0)),
        out_shape=jax.ShapeDtypeStruct((toks, width), BF16),
        scratch_shapes=[
            pltpu.VMEM((toks, experts), BF16),
            pltpu.VMEM((2 * toks, experts), BF16),
            pltpu.VMEM((2 * toks, width), F32),
        ],
        compiler_params=pltpu.CompilerParams(vmem_limit_bytes=VMEM_BYTES),
        name="combine",
    )(ids_t, quanta_t, back)


def exchange(rows, experts):
    blocks = rows.reshape(experts, SUB, rows.shape[1])
    blocks = lax.all_to_all(blocks, ("node", "local"), split_axis=0, concat_axis=0, tiled=True)
    return blocks.reshape(rows.shape)


def on_device(tokens, expert_ids, gate_quanta, w_gate, w_up, w_down):
    experts = lax.axis_size("node") * lax.axis_size("local")
    capacity = tokens.shape[0] * expert_ids.shape[1] * 9 // 8
    ids_t = expert_ids.T
    outgoing = dispatch(ids_t, tokens, experts)
    arrived = exchange(outgoing, experts)
    results = expert(arrived, w_gate[0], w_up[0], w_down[0], capacity)
    returned = exchange(results, experts)
    return combine(ids_t, gate_quanta.T, returned, experts)


def solution(mesh):
    rows = P(("node", "local"), None)
    weights = P(("node", "local"), None, None)
    return jax.shard_map(
        on_device,
        mesh=mesh,
        in_specs=(rows, rows, rows, weights, weights, weights),
        out_specs=rows,
        check_vma=False,
    )
```

```python
import jax
import jax.numpy as jnp
from jax import lax
from jax.experimental import pallas as pl
from jax.experimental.pallas import tpu as pltpu
from jax.sharding import PartitionSpec as P

AXES = ("node", "local")
ROUTED_SCALE = 2.5
SUB = 8
PARTS_A = ((0, 2), (4, 4))
PARTS_B = ((6, 2),)
LANES = 128
ROWS = 256
VMEM_BYTES = 58 * 1024 * 1024
BF16 = jnp.bfloat16
F32 = jnp.float32


def _iota(shape, dim):
    return lax.broadcasted_iota(jnp.int32, shape, dim)


def _dot(a, b):
    return jnp.dot(a, b, preferred_element_type=F32)


def _params():
    return pltpu.CompilerParams(vmem_limit_bytes=VMEM_BYTES)


def _whole(a):
    return pl.BlockSpec(a.shape, lambda i: (0, 0))


def _columns(parts, width):
    return sum(width // pieces for first, pieces in parts)


def _fill(parts, rank_rep, tokens_ref, out_ref):
    rows, toks = rank_rep.shape
    width = tokens_ref.shape[1]
    sub = _iota((rows, toks), 0) % SUB
    col = 0
    for first, pieces in parts:
        piece = width // pieces
        mine = rank_rep == first + sub // pieces
        acc = None
        for c in range(pieces):
            term = _dot((mine & (sub % pieces == c)).astype(BF16), tokens_ref[:, c * piece : (c + 1) * piece])
            acc = term if acc is None else acc + term
        out_ref[:, col : col + piece] = acc.astype(BF16)
        col += piece


def _spread(rows, experts, step):
    row = _iota((rows, experts), 0) + step * rows
    return (row // SUB == _iota((rows, experts), 1)).astype(BF16)


def dispatch_a_body(ids_t_ref, tokens_ref, out_ref, rank_ref, count_ref):
    experts, toks = rank_ref.shape
    step = pl.program_id(0)

    @pl.when(step == 0)
    def _():
        row = _iota((experts, toks), 0)
        chosen = jnp.zeros((experts, toks), F32)
        for k in range(ids_t_ref.shape[0]):
            chosen = chosen + (ids_t_ref[k : k + 1, :] == row).astype(F32)
        before = (_iota((toks, toks), 0) < _iota((toks, toks), 1)).astype(BF16)
        picked = chosen.astype(BF16)
        rank_ref[...] = jnp.where(chosen > 0, _dot(picked, before), -1.0).astype(BF16)
        count_ref[...] = _dot(picked, jnp.ones((toks, LANES), BF16)).astype(BF16)

    spread = _spread(out_ref.shape[0], experts, step)
    _fill(PARTS_A, _dot(spread, rank_ref[...]).astype(jnp.int32), tokens_ref, out_ref)
    out_ref[:, out_ref.shape[1] - LANES :] = _dot(spread, count_ref[...]).astype(BF16)


def dispatch_a(ids_t, tokens, experts):
    toks, width = tokens.shape
    cols = _columns(PARTS_A, width) + LANES
    return pl.pallas_call(
        dispatch_a_body,
        grid=(experts * SUB // ROWS,),
        in_specs=[_whole(ids_t), _whole(tokens)],
        out_specs=[
            pl.BlockSpec((ROWS, cols), lambda i: (i, 0)),
            pl.BlockSpec((experts, toks), lambda i: (0, 0)),
        ],
        out_shape=[
            jax.ShapeDtypeStruct((experts * SUB, cols), BF16),
            jax.ShapeDtypeStruct((experts, toks), BF16),
        ],
        scratch_shapes=[pltpu.VMEM((experts, LANES), BF16)],
        compiler_params=_params(),
        name="dispatch_a",
    )(ids_t, tokens)


def dispatch_b_body(rank_ref, tokens_ref, out_ref):
    spread = _spread(out_ref.shape[0], rank_ref.shape[0], pl.program_id(0))
    _fill(PARTS_B, _dot(spread, rank_ref[...]).astype(jnp.int32), tokens_ref, out_ref)


def dispatch_b(ranks, tokens):
    experts = ranks.shape[0]
    cols = _columns(PARTS_B, tokens.shape[1])
    return pl.pallas_call(
        dispatch_b_body,
        grid=(experts * SUB // ROWS,),
        in_specs=[_whole(ranks), _whole(tokens)],
        out_specs=pl.BlockSpec((ROWS, cols), lambda i: (i, 0)),
        out_shape=jax.ShapeDtypeStruct((experts * SUB, cols), BF16),
        compiler_params=_params(),
        name="dispatch_b",
    )(ranks, tokens)


def _regroup(pieces, back):
    per = ROWS // pieces
    src, dst = _iota((ROWS, ROWS), 1), _iota((ROWS, ROWS), 0)
    if back:
        src, dst = dst, src
    return (src == (dst % per) * pieces + dst // per).astype(BF16)


def expert_body(parts, capacity, arrived_ref, counts_ref, gate_ref, up_ref, down_ref, out_ref, x_ref, h_ref, y_ref, kept_ref):
    total = counts_ref.shape[0]
    rows, width = x_ref.shape
    cols = gate_ref.shape[1]
    out_cols = down_ref.shape[1]
    steps = h_ref.shape[1] // cols
    i = pl.program_id(0)

    def blocks(pieces, base):
        per = ROWS // pieces
        return [(slice(b * ROWS, (b + 1) * ROWS), base + b * per, per) for b in range(total // ROWS)]

    @pl.when(i == 0)
    def _():
        base, col = 0, 0
        for first, pieces in parts:
            piece, slots = width // pieces, SUB // pieces
            order = _regroup(pieces, False)
            for sub_rows, at, per in blocks(pieces, base):
                sorted_rows = _dot(order, arrived_ref[sub_rows, col : col + piece]).astype(BF16)
                for c in range(pieces):
                    x_ref[at : at + per, c * piece : (c + 1) * piece] = sorted_rows[c * per : (c + 1) * per]
            count = total // pieces
            row, src = _iota((count, total), 0), _iota((count, total), 1)
            earlier = ((src % SUB == 0) & (src // SUB < row // slots)).astype(BF16)
            slot = first + _iota((count, LANES), 0) % slots
            position = _dot(earlier, counts_ref[...]) + slot.astype(F32)
            kept_ref[base : base + count, :] = (position < capacity).astype(F32)
            base, col = base + count, col + piece

    @pl.when(i < steps)
    def _():
        gate = _dot(x_ref[...], gate_ref[...])
        h = 0.5 * gate * (1.0 + jnp.tanh(0.5 * gate)) * _dot(x_ref[...], up_ref[...])
        kept = jnp.concatenate([kept_ref[...]] * (cols // LANES), axis=1)
        h_ref[:, pl.ds(pl.multiple_of(i * cols, LANES), cols)] = jnp.where(kept > 0, h, 0.0).astype(BF16)

    @pl.when(i >= steps)
    def _():
        y = _dot(h_ref[...], down_ref[...]).astype(BF16)
        y_ref[:, pl.ds(pl.multiple_of((i - steps) * out_cols, LANES), out_cols)] = y

    @pl.when(i == pl.num_programs(0) - 1)
    def _():
        base, col = 0, 0
        for first, pieces in parts:
            piece = width // pieces
            order = _regroup(pieces, True)
            for sub_rows, at, per in blocks(pieces, base):
                stacked = [y_ref[at : at + per, c * piece : (c + 1) * piece] for c in range(pieces)]
                out_ref[sub_rows, col : col + piece] = _dot(order, jnp.concatenate(stacked, axis=0)).astype(BF16)
            base, col = base + total // pieces, col + piece


def expert(parts, arrived, counted, w_gate, w_up, w_down, capacity, name):
    total = arrived.shape[0]
    width, hid = w_gate.shape
    rows = sum(total // pieces for first, pieces in parts)
    cols, out_cols = 256, 512
    steps = hid // cols
    out_width = _columns(parts, width)
    counts_at = counted.shape[1] // LANES - 1
    hidden_block = pl.BlockSpec((width, cols), lambda i: (0, jnp.minimum(i, steps - 1)))

    def body(*refs):
        expert_body(parts, float(capacity), *refs)

    return pl.pallas_call(
        body,
        grid=(steps + width // out_cols,),
        in_specs=[
            pl.BlockSpec(arrived.shape, lambda i: (0, 0), pipeline_mode=pl.Buffered(1)),
            pl.BlockSpec((total, LANES), lambda i: (0, counts_at), pipeline_mode=pl.Buffered(1)),
            hidden_block,
            hidden_block,
            pl.BlockSpec((hid, out_cols), lambda i: (0, jnp.maximum(i - steps, 0))),
        ],
        out_specs=pl.BlockSpec((total, out_width), lambda i: (0, 0)),
        out_shape=jax.ShapeDtypeStruct((total, out_width), BF16),
        scratch_shapes=[
            pltpu.VMEM((rows, width), BF16),
            pltpu.VMEM((rows, hid), BF16),
            pltpu.VMEM((rows, width), BF16),
            pltpu.VMEM((rows, LANES), F32),
        ],
        compiler_params=_params(),
        cost_estimate=pl.CostEstimate(
            flops=6 * rows * width * hid, transcendentals=rows * hid, bytes_accessed=6 * width * hid + 4 * rows * width
        ),
        name=name,
    )(arrived, counted, w_gate, w_up, w_down)


def _weights(parts, rank, gate, out_refs):
    toks, experts = rank.shape
    subs = experts * SUB
    spread = (_iota((experts, subs), 1) // SUB == _iota((experts, subs), 0)).astype(BF16)
    rank = _dot(rank, spread).astype(jnp.int32)
    rank = jnp.concatenate([rank, rank], axis=0)
    gate = _dot(gate, spread)
    sub = _iota((2 * toks, subs), 1) % SUB
    for (first, pieces), out_ref in zip(parts, out_refs):
        weight = jnp.where(rank == first + sub // pieces, gate, 0.0)
        for c in range(pieces):
            out_ref[c] = jnp.where(sub % pieces == c, weight, 0.0).astype(BF16)


def _column(i):
    return (i % 2) * 2 + i // 2


def combine_a_body(ids_t_ref, quanta_t_ref, ranks_ref, half_ref, quarter_ref, out_ref, later_ref, half_w, quarter_w):
    toks = out_ref.shape[0]
    experts = ranks_ref.shape[0]
    i = pl.program_id(0)

    @pl.when(i == 0)
    def _():
        rank = ranks_ref[...].astype(F32).T.astype(BF16)
        quanta = quanta_t_ref[...].astype(F32)
        scale = ROUTED_SCALE * quanta / jnp.sum(quanta, axis=0, keepdims=True)
        row = _iota((experts, toks), 0)
        gate = jnp.zeros((experts, toks), F32)
        for k in range(ids_t_ref.shape[0]):
            gate = gate + jnp.where(ids_t_ref[k : k + 1, :] == row, scale[k : k + 1, :], 0.0)
        gate = gate.T
        high = gate.astype(BF16)
        gate = jnp.concatenate([high, (gate - high.astype(F32)).astype(BF16)], axis=0)
        _weights(PARTS_A, rank, gate, (half_w, quarter_w))
        _weights(PARTS_B, rank, gate, (later_ref,))

    total = _dot(half_w[i % 2], half_ref[...]) + _dot(quarter_w[_column(i)], quarter_ref[...])
    out_ref[...] = total[0:toks] + total[toks:]


def combine_a(ids_t, quanta_t, ranks, back, width):
    experts, toks = ranks.shape
    subs = back.shape[0]
    quarter = width // 4
    return pl.pallas_call(
        combine_a_body,
        grid=(4,),
        in_specs=[
            _whole(ids_t),
            _whole(quanta_t),
            _whole(ranks),
            pl.BlockSpec((subs, quarter), lambda i: (0, i // 2)),
            pl.BlockSpec((subs, quarter), lambda i: (0, 2)),
        ],
        out_specs=[
            pl.BlockSpec((toks, quarter), lambda i: (0, _column(i))),
            pl.BlockSpec((2, 2 * toks, subs), lambda i: (0, 0, 0)),
        ],
        out_shape=[
            jax.ShapeDtypeStruct((toks, width), F32),
            jax.ShapeDtypeStruct((2, 2 * toks, subs), BF16),
        ],
        scratch_shapes=[pltpu.VMEM((2, 2 * toks, subs), BF16), pltpu.VMEM((4, 2 * toks, subs), BF16)],
        compiler_params=_params(),
        name="combine_a",
    )(ids_t, quanta_t, ranks, back, back)


def combine_b_body(sum_ref, weight_ref, half_ref, out_ref):
    toks = out_ref.shape[0]
    total = _dot(weight_ref[pl.program_id(0) % 2], half_ref[...])
    out_ref[...] = (sum_ref[...] + total[0:toks] + total[toks:]).astype(BF16)


def combine_b(partial, weight, back):
    toks, width = partial.shape
    quarter = width // 4
    block = pl.BlockSpec((toks, quarter), lambda i: (0, _column(i)))
    return pl.pallas_call(
        combine_b_body,
        grid=(4,),
        in_specs=[
            block,
            pl.BlockSpec(weight.shape, lambda i: (0, 0, 0)),
            pl.BlockSpec((back.shape[0], quarter), lambda i: (0, i // 2)),
        ],
        out_specs=block,
        out_shape=jax.ShapeDtypeStruct((toks, width), BF16),
        compiler_params=_params(),
        name="combine_b",
    )(partial, weight, back)


def exchange(rows):
    blocks = rows.reshape(rows.shape[0] // SUB, SUB, rows.shape[1])
    blocks = lax.all_to_all(blocks, AXES, split_axis=0, concat_axis=0, tiled=True)
    return blocks.reshape(rows.shape)


def on_device(tokens, expert_ids, gate_quanta, w_gate, w_up, w_down):
    experts = lax.axis_size("node") * lax.axis_size("local")
    capacity = tokens.shape[0] * expert_ids.shape[1] * 9 // 8
    ids_t = expert_ids.T
    weights = (w_gate[0], w_up[0], w_down[0])
    out_a, ranks = dispatch_a(ids_t, tokens, experts)
    in_a = exchange(out_a)
    out_b = dispatch_b(ranks, tokens)
    in_a, out_b = lax.optimization_barrier((in_a, out_b))
    in_b = exchange(out_b)
    done_a = expert(PARTS_A, in_a, in_a, *weights, capacity, "expert_a")
    back_a = exchange(done_a)
    done_b = expert(PARTS_B, in_b, in_a, *weights, capacity, "expert_b")
    back_a, done_b = lax.optimization_barrier((back_a, done_b))
    back_b = exchange(done_b)
    partial, weight = combine_a(ids_t, gate_quanta.T, ranks, back_a, tokens.shape[1])
    return combine_b(partial, weight, back_b)


def solution(mesh):
    rows = P(AXES, None)
    weights = P(AXES, None, None)
    return jax.shard_map(
        on_device,
        mesh=mesh,
        in_specs=(rows, rows, rows, weights, weights, weights),
        out_specs=rows,
        check_vma=False,
    )
```

```python
import jax
import jax.numpy as jnp
from jax import lax
from jax.experimental import pallas as pl
from jax.experimental.pallas import tpu as pltpu
from jax.sharding import PartitionSpec as P

AXES = ("node", "local")
ROUTED_SCALE = 2.5
SUB = 8
PARTS_A = ((0, 2), (4, 4))
PARTS_B = ((6, 2),)
LANES = 128
ROWS = 256
VMEM_BYTES = 58 * 1024 * 1024
BF16 = jnp.bfloat16
F32 = jnp.float32


def _iota(shape, dim):
    return lax.broadcasted_iota(jnp.int32, shape, dim)


def _dot(a, b):
    return jnp.dot(a, b, preferred_element_type=F32)


def _params():
    return pltpu.CompilerParams(vmem_limit_bytes=VMEM_BYTES)


def _whole(a):
    return pl.BlockSpec(a.shape, lambda i: (0, 0))


def _columns(parts, width):
    return sum(width // pieces for first, pieces in parts)


def _stack(parts, tokens_ref, stack_refs):
    toks, width = tokens_ref.shape
    for (first, pieces), stack_ref in zip(parts, stack_refs):
        piece = width // pieces
        for c in range(pieces):
            stack_ref[c * toks : (c + 1) * toks, :] = tokens_ref[:, c * piece : (c + 1) * piece]


def _stack_shapes(parts, toks, width):
    return [pltpu.VMEM((pieces * toks, width // pieces), BF16) for first, pieces in parts]


def _fill(parts, rank_rep, stack_refs, out_ref):
    sub = _iota(rank_rep.shape, 0) % SUB
    col = 0
    for (first, pieces), stack_ref in zip(parts, stack_refs):
        mine = jnp.where(rank_rep == first + sub // pieces, sub % pieces, -1)
        pick = jnp.concatenate([(mine == c).astype(F32) for c in range(pieces)], axis=1).astype(BF16)
        piece = stack_ref.shape[1]
        out_ref[:, col : col + piece] = _dot(pick, stack_ref[...]).astype(BF16)
        col += piece


def _spread(rows, experts, step):
    row = _iota((rows, experts), 0) + step * rows
    return (row // SUB == _iota((rows, experts), 1)).astype(BF16)


def dispatch_a_body(ids_t_ref, tokens_ref, out_ref, rank_ref, count_ref, *stack_refs):
    experts, toks = rank_ref.shape
    step = pl.program_id(0)

    @pl.when(step == 0)
    def _():
        row = _iota((experts, toks), 0)
        chosen = jnp.zeros((experts, toks), F32)
        for k in range(ids_t_ref.shape[0]):
            chosen = chosen + (ids_t_ref[k : k + 1, :] == row).astype(F32)
        before = (_iota((toks, toks), 0) < _iota((toks, toks), 1)).astype(BF16)
        picked = chosen.astype(BF16)
        rank_ref[...] = jnp.where(chosen > 0, _dot(picked, before), -1.0).astype(BF16)
        count_ref[...] = _dot(picked, jnp.ones((toks, LANES), BF16)).astype(BF16)
        _stack(PARTS_A, tokens_ref, stack_refs)

    spread = _spread(out_ref.shape[0], experts, step)
    _fill(PARTS_A, _dot(spread, rank_ref[...]).astype(jnp.int32), stack_refs, out_ref)
    out_ref[:, out_ref.shape[1] - LANES :] = _dot(spread, count_ref[...]).astype(BF16)


def dispatch_a(ids_t, tokens, experts):
    toks, width = tokens.shape
    cols = _columns(PARTS_A, width) + LANES
    return pl.pallas_call(
        dispatch_a_body,
        grid=(experts * SUB // ROWS,),
        in_specs=[_whole(ids_t), _whole(tokens)],
        out_specs=[
            pl.BlockSpec((ROWS, cols), lambda i: (i, 0)),
            pl.BlockSpec((experts, toks), lambda i: (0, 0)),
        ],
        out_shape=[
            jax.ShapeDtypeStruct((experts * SUB, cols), BF16),
            jax.ShapeDtypeStruct((experts, toks), BF16),
        ],
        scratch_shapes=[pltpu.VMEM((experts, LANES), BF16), *_stack_shapes(PARTS_A, toks, width)],
        compiler_params=_params(),
        name="dispatch_a",
    )(ids_t, tokens)


def dispatch_b_body(rank_ref, tokens_ref, out_ref, *stack_refs):
    @pl.when(pl.program_id(0) == 0)
    def _():
        _stack(PARTS_B, tokens_ref, stack_refs)

    spread = _spread(out_ref.shape[0], rank_ref.shape[0], pl.program_id(0))
    _fill(PARTS_B, _dot(spread, rank_ref[...]).astype(jnp.int32), stack_refs, out_ref)


def dispatch_b(ranks, tokens):
    experts = ranks.shape[0]
    cols = _columns(PARTS_B, tokens.shape[1])
    return pl.pallas_call(
        dispatch_b_body,
        grid=(experts * SUB // ROWS,),
        in_specs=[_whole(ranks), _whole(tokens)],
        out_specs=pl.BlockSpec((ROWS, cols), lambda i: (i, 0)),
        out_shape=jax.ShapeDtypeStruct((experts * SUB, cols), BF16),
        scratch_shapes=_stack_shapes(PARTS_B, *tokens.shape),
        compiler_params=_params(),
        name="dispatch_b",
    )(ranks, tokens)


def _regroup(pieces, back):
    per = ROWS // pieces
    src, dst = _iota((ROWS, ROWS), 1), _iota((ROWS, ROWS), 0)
    if back:
        src, dst = dst, src
    return (src == (dst % per) * pieces + dst // per).astype(BF16)


def expert_body(parts, capacity, arrived_ref, counts_ref, gate_ref, up_ref, down_ref, out_ref, x_ref, h_ref, y_ref, kept_ref):
    total = counts_ref.shape[0]
    rows, width = x_ref.shape
    cols = gate_ref.shape[1]
    out_cols = down_ref.shape[1]
    steps = h_ref.shape[1] // cols
    i = pl.program_id(0)

    def blocks(pieces, base):
        per = ROWS // pieces
        return [(slice(b * ROWS, (b + 1) * ROWS), base + b * per, per) for b in range(total // ROWS)]

    @pl.when(i == 0)
    def _():
        base, col = 0, 0
        for first, pieces in parts:
            piece, slots = width // pieces, SUB // pieces
            order = _regroup(pieces, False)
            for sub_rows, at, per in blocks(pieces, base):
                sorted_rows = _dot(order, arrived_ref[sub_rows, col : col + piece]).astype(BF16)
                for c in range(pieces):
                    x_ref[at : at + per, c * piece : (c + 1) * piece] = sorted_rows[c * per : (c + 1) * per]
            count = total // pieces
            row, src = _iota((count, total), 0), _iota((count, total), 1)
            earlier = ((src % SUB == 0) & (src // SUB < row // slots)).astype(BF16)
            slot = first + _iota((count, LANES), 0) % slots
            position = _dot(earlier, counts_ref[...]) + slot.astype(F32)
            kept_ref[base : base + count, :] = (position < capacity).astype(F32)
            base, col = base + count, col + piece

    @pl.when(i < steps)
    def _():
        gate = _dot(x_ref[...], gate_ref[...])
        h = 0.5 * gate * (1.0 + jnp.tanh(0.5 * gate)) * _dot(x_ref[...], up_ref[...])
        kept = jnp.concatenate([kept_ref[...]] * (cols // LANES), axis=1)
        h_ref[:, pl.ds(pl.multiple_of(i * cols, LANES), cols)] = jnp.where(kept > 0, h, 0.0).astype(BF16)

    @pl.when(i >= steps)
    def _():
        y = _dot(h_ref[...], down_ref[...]).astype(BF16)
        y_ref[:, pl.ds(pl.multiple_of((i - steps) * out_cols, LANES), out_cols)] = y

    @pl.when(i == pl.num_programs(0) - 1)
    def _():
        base, col = 0, 0
        for first, pieces in parts:
            piece = width // pieces
            order = _regroup(pieces, True)
            for sub_rows, at, per in blocks(pieces, base):
                stacked = [y_ref[at : at + per, c * piece : (c + 1) * piece] for c in range(pieces)]
                out_ref[sub_rows, col : col + piece] = _dot(order, jnp.concatenate(stacked, axis=0)).astype(BF16)
            base, col = base + total // pieces, col + piece


def expert(parts, arrived, counted, w_gate, w_up, w_down, capacity, name):
    total = arrived.shape[0]
    width, hid = w_gate.shape
    rows = sum(total // pieces for first, pieces in parts)
    cols, out_cols = 256, 512
    steps = hid // cols
    out_width = _columns(parts, width)
    counts_at = counted.shape[1] // LANES - 1
    hidden_block = pl.BlockSpec((width, cols), lambda i: (0, jnp.minimum(i, steps - 1)))

    def body(*refs):
        expert_body(parts, float(capacity), *refs)

    return pl.pallas_call(
        body,
        grid=(steps + width // out_cols,),
        in_specs=[
            pl.BlockSpec(arrived.shape, lambda i: (0, 0), pipeline_mode=pl.Buffered(1)),
            pl.BlockSpec((total, LANES), lambda i: (0, counts_at), pipeline_mode=pl.Buffered(1)),
            hidden_block,
            hidden_block,
            pl.BlockSpec((hid, out_cols), lambda i: (0, jnp.maximum(i - steps, 0))),
        ],
        out_specs=pl.BlockSpec((total, out_width), lambda i: (0, 0)),
        out_shape=jax.ShapeDtypeStruct((total, out_width), BF16),
        scratch_shapes=[
            pltpu.VMEM((rows, width), BF16),
            pltpu.VMEM((rows, hid), BF16),
            pltpu.VMEM((rows, width), BF16),
            pltpu.VMEM((rows, LANES), F32),
        ],
        compiler_params=_params(),
        cost_estimate=pl.CostEstimate(
            flops=6 * rows * width * hid, transcendentals=rows * hid, bytes_accessed=6 * width * hid + 4 * rows * width
        ),
        name=name,
    )(arrived, counted, w_gate, w_up, w_down)


def _weights(parts, rank, gate, out_refs):
    toks, experts = rank.shape
    subs = experts * SUB
    spread = (_iota((experts, subs), 1) // SUB == _iota((experts, subs), 0)).astype(BF16)
    rank = _dot(rank, spread).astype(jnp.int32)
    rank = jnp.concatenate([rank, rank], axis=0)
    gate = _dot(gate, spread)
    sub = _iota((2 * toks, subs), 1) % SUB
    for (first, pieces), out_ref in zip(parts, out_refs):
        weight = jnp.where(rank == first + sub // pieces, gate, 0.0)
        for c in range(pieces):
            out_ref[c] = jnp.where(sub % pieces == c, weight, 0.0).astype(BF16)


def _column(i):
    return (i % 2) * 2 + i // 2


def combine_a_body(ids_t_ref, quanta_t_ref, ranks_ref, half_ref, quarter_ref, out_ref, later_ref, half_w, quarter_w):
    toks = out_ref.shape[0]
    experts = ranks_ref.shape[0]
    i = pl.program_id(0)

    @pl.when(i == 0)
    def _():
        rank = ranks_ref[...].astype(F32).T.astype(BF16)
        quanta = quanta_t_ref[...].astype(F32)
        scale = ROUTED_SCALE * quanta / jnp.sum(quanta, axis=0, keepdims=True)
        row = _iota((experts, toks), 0)
        gate = jnp.zeros((experts, toks), F32)
        for k in range(ids_t_ref.shape[0]):
            gate = gate + jnp.where(ids_t_ref[k : k + 1, :] == row, scale[k : k + 1, :], 0.0)
        gate = gate.T
        high = gate.astype(BF16)
        gate = jnp.concatenate([high, (gate - high.astype(F32)).astype(BF16)], axis=0)
        _weights(PARTS_A, rank, gate, (half_w, quarter_w))
        _weights(PARTS_B, rank, gate, (later_ref,))

    total = _dot(half_w[i % 2], half_ref[...]) + _dot(quarter_w[_column(i)], quarter_ref[...])
    out_ref[...] = total[0:toks] + total[toks:]


def combine_a(ids_t, quanta_t, ranks, back, width):
    experts, toks = ranks.shape
    subs = back.shape[0]
    quarter = width // 4
    return pl.pallas_call(
        combine_a_body,
        grid=(4,),
        in_specs=[
            _whole(ids_t),
            _whole(quanta_t),
            _whole(ranks),
            pl.BlockSpec((subs, quarter), lambda i: (0, i // 2)),
            pl.BlockSpec((subs, quarter), lambda i: (0, 2)),
        ],
        out_specs=[
            pl.BlockSpec((toks, quarter), lambda i: (0, _column(i))),
            pl.BlockSpec((2, 2 * toks, subs), lambda i: (0, 0, 0)),
        ],
        out_shape=[
            jax.ShapeDtypeStruct((toks, width), F32),
            jax.ShapeDtypeStruct((2, 2 * toks, subs), BF16),
        ],
        scratch_shapes=[pltpu.VMEM((2, 2 * toks, subs), BF16), pltpu.VMEM((4, 2 * toks, subs), BF16)],
        compiler_params=_params(),
        name="combine_a",
    )(ids_t, quanta_t, ranks, back, back)


def combine_b_body(sum_hbm, weight_hbm, half_hbm, out_hbm, sum_ref, weight_ref, half_ref, out_ref, in_sems, out_sems):
    toks, quarter = out_ref.shape[1:]

    def columns(q):
        return pl.ds(q * quarter, quarter)

    weights = [pltpu.make_async_copy(weight_hbm.at[h], weight_ref.at[h], in_sems.at[h]) for h in range(2)]
    halves = [pltpu.make_async_copy(half_hbm.at[:, columns(h)], half_ref.at[h], in_sems.at[2 + h]) for h in range(2)]
    sums = [pltpu.make_async_copy(sum_hbm.at[:, columns(q)], sum_ref.at[q], in_sems.at[4 + q]) for q in range(4)]
    outs = [pltpu.make_async_copy(out_ref.at[q], out_hbm.at[:, columns(q)], out_sems.at[q]) for q in range(4)]
    for copy in (halves[0], weights[0], sums[0], weights[1], sums[2], halves[1], sums[1], sums[3]):
        copy.start()
    for q in (0, 2, 1, 3):
        h, side = q // 2, q % 2
        if h == 0:
            halves[side].wait()
        if side == 0:
            weights[h].wait()
        total = _dot(weight_ref[h], half_ref[side])
        sums[q].wait()
        out_ref[q] = (sum_ref[q] + total[0:toks] + total[toks:]).astype(BF16)
        outs[q].start()
    for q in range(4):
        outs[q].wait()


def combine_b(partial, weight, back):
    toks, width = partial.shape
    quarter = width // 4
    anywhere = pl.BlockSpec(memory_space=pl.ANY)
    return pl.pallas_call(
        combine_b_body,
        in_specs=[anywhere, anywhere, anywhere],
        out_specs=anywhere,
        out_shape=jax.ShapeDtypeStruct((toks, width), BF16),
        scratch_shapes=[
            pltpu.VMEM((4, toks, quarter), F32),
            pltpu.VMEM(weight.shape, BF16),
            pltpu.VMEM((2, back.shape[0], quarter), BF16),
            pltpu.VMEM((4, toks, quarter), BF16),
            pltpu.SemaphoreType.DMA((8,)),
            pltpu.SemaphoreType.DMA((4,)),
        ],
        compiler_params=_params(),
        name="combine_b",
    )(partial, weight, back)


def exchange(rows):
    blocks = rows.reshape(rows.shape[0] // SUB, SUB, rows.shape[1])
    blocks = lax.all_to_all(blocks, AXES, split_axis=0, concat_axis=0, tiled=True)
    return blocks.reshape(rows.shape)


def on_device(tokens, expert_ids, gate_quanta, w_gate, w_up, w_down):
    experts = lax.axis_size("node") * lax.axis_size("local")
    capacity = tokens.shape[0] * expert_ids.shape[1] * 9 // 8
    ids_t = expert_ids.T
    weights = (w_gate[0], w_up[0], w_down[0])
    out_a, ranks = dispatch_a(ids_t, tokens, experts)
    in_a = exchange(out_a)
    out_b = dispatch_b(ranks, tokens)
    in_a, out_b = lax.optimization_barrier((in_a, out_b))
    in_b = exchange(out_b)
    done_a = expert(PARTS_A, in_a, in_a, *weights, capacity, "expert_a")
    back_a = exchange(done_a)
    done_b = expert(PARTS_B, in_b, in_a, *weights, capacity, "expert_b")
    back_a, done_b = lax.optimization_barrier((back_a, done_b))
    back_b = exchange(done_b)
    partial, weight = combine_a(ids_t, gate_quanta.T, ranks, back_a, tokens.shape[1])
    return combine_b(partial, weight, back_b)


def solution(mesh):
    rows = P(AXES, None)
    weights = P(AXES, None, None)
    return jax.shard_map(
        on_device,
        mesh=mesh,
        in_specs=(rows, rows, rows, weights, weights, weights),
        out_specs=rows,
        check_vma=False,
    )
```

```python
import jax
import jax.numpy as jnp
from jax import lax
from jax.experimental import pallas as pl
from jax.experimental.pallas import tpu as pltpu
from jax.sharding import PartitionSpec as P

AXES = ("node", "local")
ROUTED_SCALE = 2.5
SUB = 8
PARTS_A = ((0, 2), (4, 4))
PARTS_B = ((6, 2),)
LANES = 128
ROWS = 256
DISPATCH_ROWS = 512
VMEM_BYTES = 58 * 1024 * 1024
BF16 = jnp.bfloat16
F32 = jnp.float32


def _iota(shape, dim):
    return lax.broadcasted_iota(jnp.int32, shape, dim)


def _dot(a, b):
    return jnp.dot(a, b, preferred_element_type=F32)


def _params():
    return pltpu.CompilerParams(vmem_limit_bytes=VMEM_BYTES)


def _whole(a):
    return pl.BlockSpec(a.shape, lambda i: (0, 0))


def _columns(parts, width):
    return sum(width // pieces for first, pieces in parts)


def _stack(parts, tokens_ref, stack_refs):
    toks, width = tokens_ref.shape
    for (first, pieces), stack_ref in zip(parts, stack_refs):
        piece = width // pieces
        for c in range(pieces):
            stack_ref[c * toks : (c + 1) * toks, :] = tokens_ref[:, c * piece : (c + 1) * piece]


def _stack_shapes(parts, toks, width):
    return [pltpu.VMEM((pieces * toks, width // pieces), BF16) for first, pieces in parts]


def _fill(parts, rank_rep, stack_refs, out_ref):
    sub = _iota(rank_rep.shape, 0) % SUB
    col = 0
    for (first, pieces), stack_ref in zip(parts, stack_refs):
        mine = jnp.where(rank_rep == first + sub // pieces, sub % pieces, -1)
        pick = jnp.concatenate([(mine == c).astype(F32) for c in range(pieces)], axis=1).astype(BF16)
        piece = stack_ref.shape[1]
        out_ref[:, col : col + piece] = _dot(pick, stack_ref[...]).astype(BF16)
        col += piece


def _spread(rows, experts, step):
    row = _iota((rows, experts), 0) + step * rows
    return (row // SUB == _iota((rows, experts), 1)).astype(BF16)


def dispatch_a_body(ids_t_ref, tokens_ref, out_ref, rank_ref, count_ref, *stack_refs):
    experts, toks = rank_ref.shape
    step = pl.program_id(0)

    @pl.when(step == 0)
    def _():
        row = _iota((experts, toks), 0)
        chosen = jnp.zeros((experts, toks), F32)
        for k in range(ids_t_ref.shape[0]):
            chosen = chosen + (ids_t_ref[k : k + 1, :] == row).astype(F32)
        before = (_iota((toks, toks), 0) < _iota((toks, toks), 1)).astype(BF16)
        picked = chosen.astype(BF16)
        rank_ref[...] = jnp.where(chosen > 0, _dot(picked, before), -1.0).astype(BF16)
        count_ref[...] = _dot(picked, jnp.ones((toks, LANES), BF16)).astype(BF16)
        _stack(PARTS_A, tokens_ref, stack_refs)

    spread = _spread(out_ref.shape[0], experts, step)
    _fill(PARTS_A, _dot(spread, rank_ref[...]).astype(jnp.int32), stack_refs, out_ref)
    out_ref[:, out_ref.shape[1] - LANES :] = _dot(spread, count_ref[...]).astype(BF16)


def dispatch_a(ids_t, tokens, experts):
    toks, width = tokens.shape
    cols = _columns(PARTS_A, width) + LANES
    return pl.pallas_call(
        dispatch_a_body,
        grid=(experts * SUB // DISPATCH_ROWS,),
        in_specs=[_whole(ids_t), _whole(tokens)],
        out_specs=[
            pl.BlockSpec((DISPATCH_ROWS, cols), lambda i: (i, 0)),
            pl.BlockSpec((experts, toks), lambda i: (0, 0)),
        ],
        out_shape=[
            jax.ShapeDtypeStruct((experts * SUB, cols), BF16),
            jax.ShapeDtypeStruct((experts, toks), BF16),
        ],
        scratch_shapes=[pltpu.VMEM((experts, LANES), BF16), *_stack_shapes(PARTS_A, toks, width)],
        compiler_params=_params(),
        name="dispatch_a",
    )(ids_t, tokens)


def dispatch_b_body(rank_ref, tokens_ref, out_ref, *stack_refs):
    @pl.when(pl.program_id(0) == 0)
    def _():
        _stack(PARTS_B, tokens_ref, stack_refs)

    spread = _spread(out_ref.shape[0], rank_ref.shape[0], pl.program_id(0))
    _fill(PARTS_B, _dot(spread, rank_ref[...]).astype(jnp.int32), stack_refs, out_ref)


def dispatch_b(ranks, tokens):
    experts = ranks.shape[0]
    cols = _columns(PARTS_B, tokens.shape[1])
    return pl.pallas_call(
        dispatch_b_body,
        grid=(experts * SUB // DISPATCH_ROWS,),
        in_specs=[_whole(ranks), _whole(tokens)],
        out_specs=pl.BlockSpec((DISPATCH_ROWS, cols), lambda i: (i, 0)),
        out_shape=jax.ShapeDtypeStruct((experts * SUB, cols), BF16),
        scratch_shapes=_stack_shapes(PARTS_B, *tokens.shape),
        compiler_params=_params(),
        name="dispatch_b",
    )(ranks, tokens)


def _regroup(pieces, back):
    per = ROWS // pieces
    src, dst = _iota((ROWS, ROWS), 1), _iota((ROWS, ROWS), 0)
    if back:
        src, dst = dst, src
    return (src == (dst % per) * pieces + dst // per).astype(BF16)


def expert_body(parts, capacity, arrived_ref, counts_ref, gate_ref, up_ref, down_ref, out_ref, x_ref, h_ref, y_ref, kept_ref):
    total = counts_ref.shape[0]
    rows, width = x_ref.shape
    cols = gate_ref.shape[1]
    out_cols = down_ref.shape[1]
    steps = h_ref.shape[1] // cols
    i = pl.program_id(0)

    def blocks(pieces, base):
        per = ROWS // pieces
        return [(slice(b * ROWS, (b + 1) * ROWS), base + b * per, per) for b in range(total // ROWS)]

    @pl.when(i == 0)
    def _():
        base, col = 0, 0
        for first, pieces in parts:
            piece, slots = width // pieces, SUB // pieces
            order = _regroup(pieces, False)
            for sub_rows, at, per in blocks(pieces, base):
                sorted_rows = _dot(order, arrived_ref[sub_rows, col : col + piece]).astype(BF16)
                for c in range(pieces):
                    x_ref[at : at + per, c * piece : (c + 1) * piece] = sorted_rows[c * per : (c + 1) * per]
            count = total // pieces
            row, src = _iota((count, total), 0), _iota((count, total), 1)
            earlier = ((src % SUB == 0) & (src // SUB < row // slots)).astype(BF16)
            slot = first + _iota((count, LANES), 0) % slots
            position = _dot(earlier, counts_ref[...]) + slot.astype(F32)
            kept_ref[base : base + count, :] = (position < capacity).astype(F32)
            base, col = base + count, col + piece

    @pl.when(i < steps)
    def _():
        gate = _dot(x_ref[...], gate_ref[...])
        h = 0.5 * gate * (1.0 + jnp.tanh(0.5 * gate)) * _dot(x_ref[...], up_ref[...])
        kept = jnp.concatenate([kept_ref[...]] * (cols // LANES), axis=1)
        h_ref[:, pl.ds(pl.multiple_of(i * cols, LANES), cols)] = jnp.where(kept > 0, h, 0.0).astype(BF16)

    @pl.when(i >= steps)
    def _():
        y = _dot(h_ref[...], down_ref[...]).astype(BF16)
        y_ref[:, pl.ds(pl.multiple_of((i - steps) * out_cols, LANES), out_cols)] = y

    @pl.when(i == pl.num_programs(0) - 1)
    def _():
        base, col = 0, 0
        for first, pieces in parts:
            piece = width // pieces
            order = _regroup(pieces, True)
            for sub_rows, at, per in blocks(pieces, base):
                stacked = [y_ref[at : at + per, c * piece : (c + 1) * piece] for c in range(pieces)]
                out_ref[sub_rows, col : col + piece] = _dot(order, jnp.concatenate(stacked, axis=0)).astype(BF16)
            base, col = base + total // pieces, col + piece


def expert(parts, arrived, counted, w_gate, w_up, w_down, capacity, name):
    total = arrived.shape[0]
    width, hid = w_gate.shape
    rows = sum(total // pieces for first, pieces in parts)
    cols, out_cols = 256, 512
    steps = hid // cols
    out_width = _columns(parts, width)
    counts_at = counted.shape[1] // LANES - 1
    hidden_block = pl.BlockSpec((width, cols), lambda i: (0, jnp.minimum(i, steps - 1)))

    def body(*refs):
        expert_body(parts, float(capacity), *refs)

    return pl.pallas_call(
        body,
        grid=(steps + width // out_cols,),
        in_specs=[
            pl.BlockSpec(arrived.shape, lambda i: (0, 0), pipeline_mode=pl.Buffered(1)),
            pl.BlockSpec((total, LANES), lambda i: (0, counts_at), pipeline_mode=pl.Buffered(1)),
            hidden_block,
            hidden_block,
            pl.BlockSpec((hid, out_cols), lambda i: (0, jnp.maximum(i - steps, 0))),
        ],
        out_specs=pl.BlockSpec((total, out_width), lambda i: (0, 0)),
        out_shape=jax.ShapeDtypeStruct((total, out_width), BF16),
        scratch_shapes=[
            pltpu.VMEM((rows, width), BF16),
            pltpu.VMEM((rows, hid), BF16),
            pltpu.VMEM((rows, width), BF16),
            pltpu.VMEM((rows, LANES), F32),
        ],
        compiler_params=_params(),
        cost_estimate=pl.CostEstimate(
            flops=6 * rows * width * hid, transcendentals=rows * hid, bytes_accessed=6 * width * hid + 4 * rows * width
        ),
        name=name,
    )(arrived, counted, w_gate, w_up, w_down)


def _weights(parts, rank, gate, out_refs):
    toks, experts = rank.shape
    subs = experts * SUB
    spread = (_iota((experts, subs), 1) // SUB == _iota((experts, subs), 0)).astype(BF16)
    rank = _dot(rank, spread).astype(jnp.int32)
    rank = jnp.concatenate([rank, rank], axis=0)
    gate = _dot(gate, spread)
    sub = _iota((2 * toks, subs), 1) % SUB
    for (first, pieces), out_ref in zip(parts, out_refs):
        weight = jnp.where(rank == first + sub // pieces, gate, 0.0)
        for c in range(pieces):
            out_ref[c] = jnp.where(sub % pieces == c, weight, 0.0).astype(BF16)


def _column(i):
    return (i % 2) * 2 + i // 2


def combine_a_body(ids_t_ref, quanta_t_ref, ranks_ref, half_ref, quarter_ref, out_ref, later_ref, half_w, quarter_w):
    toks = out_ref.shape[0]
    experts = ranks_ref.shape[0]
    i = pl.program_id(0)

    @pl.when(i == 0)
    def _():
        rank = ranks_ref[...].astype(F32).T.astype(BF16)
        quanta = quanta_t_ref[...].astype(F32)
        scale = ROUTED_SCALE * quanta / jnp.sum(quanta, axis=0, keepdims=True)
        row = _iota((experts, toks), 0)
        gate = jnp.zeros((experts, toks), F32)
        for k in range(ids_t_ref.shape[0]):
            gate = gate + jnp.where(ids_t_ref[k : k + 1, :] == row, scale[k : k + 1, :], 0.0)
        gate = gate.T
        high = gate.astype(BF16)
        gate = jnp.concatenate([high, (gate - high.astype(F32)).astype(BF16)], axis=0)
        _weights(PARTS_A, rank, gate, (half_w, quarter_w))
        _weights(PARTS_B, rank, gate, (later_ref,))

    total = _dot(half_w[i % 2], half_ref[...]) + _dot(quarter_w[_column(i)], quarter_ref[...])
    out_ref[...] = total[0:toks] + total[toks:]


def combine_a(ids_t, quanta_t, ranks, back, width):
    experts, toks = ranks.shape
    subs = back.shape[0]
    quarter = width // 4
    return pl.pallas_call(
        combine_a_body,
        grid=(4,),
        in_specs=[
            _whole(ids_t),
            _whole(quanta_t),
            _whole(ranks),
            pl.BlockSpec((subs, quarter), lambda i: (0, i // 2)),
            pl.BlockSpec((subs, quarter), lambda i: (0, 2)),
        ],
        out_specs=[
            pl.BlockSpec((toks, quarter), lambda i: (0, _column(i))),
            pl.BlockSpec((2, 2 * toks, subs), lambda i: (0, 0, 0)),
        ],
        out_shape=[
            jax.ShapeDtypeStruct((toks, width), F32),
            jax.ShapeDtypeStruct((2, 2 * toks, subs), BF16),
        ],
        scratch_shapes=[pltpu.VMEM((2, 2 * toks, subs), BF16), pltpu.VMEM((4, 2 * toks, subs), BF16)],
        compiler_params=_params(),
        name="combine_a",
    )(ids_t, quanta_t, ranks, back, back)


def combine_b_body(sum_hbm, weight_hbm, half_hbm, out_hbm, sum_ref, weight_ref, half_ref, out_ref, in_sems, out_sems):
    toks, quarter = out_ref.shape[1:]

    def columns(q):
        return pl.ds(q * quarter, quarter)

    weights = pltpu.make_async_copy(weight_hbm, weight_ref, in_sems.at[0])
    halves = [pltpu.make_async_copy(half_hbm.at[:, columns(h)], half_ref.at[h], in_sems.at[2 + h]) for h in range(2)]
    sums = [pltpu.make_async_copy(sum_hbm.at[:, columns(q)], sum_ref.at[q], in_sems.at[4 + q]) for q in range(4)]
    outs = [pltpu.make_async_copy(out_ref.at[q], out_hbm.at[:, columns(q)], out_sems.at[q]) for q in range(4)]
    for copy in (weights, halves[0], sums[0], sums[2], halves[1], sums[1], sums[3]):
        copy.start()
    weights.wait()
    for side in range(2):
        halves[side].wait()
        total = _dot(weight_ref[...], half_ref[side])
        for h in range(2):
            q, at = 2 * h + side, 2 * h * toks
            sums[q].wait()
            out_ref[q] = (sum_ref[q] + total[at : at + toks] + total[at + toks : at + 2 * toks]).astype(BF16)
            outs[q].start()
    for q in range(4):
        outs[q].wait()


def combine_b(partial, weight, back):
    toks, width = partial.shape
    quarter = width // 4
    weight = weight.reshape(4 * toks, back.shape[0])
    anywhere = pl.BlockSpec(memory_space=pl.ANY)
    return pl.pallas_call(
        combine_b_body,
        in_specs=[anywhere, anywhere, anywhere],
        out_specs=anywhere,
        out_shape=jax.ShapeDtypeStruct((toks, width), BF16),
        scratch_shapes=[
            pltpu.VMEM((4, toks, quarter), F32),
            pltpu.VMEM(weight.shape, BF16),
            pltpu.VMEM((2, back.shape[0], quarter), BF16),
            pltpu.VMEM((4, toks, quarter), BF16),
            pltpu.SemaphoreType.DMA((8,)),
            pltpu.SemaphoreType.DMA((4,)),
        ],
        compiler_params=_params(),
        name="combine_b",
    )(partial, weight, back)


def exchange(rows):
    blocks = rows.reshape(rows.shape[0] // SUB, SUB, rows.shape[1])
    blocks = lax.all_to_all(blocks, AXES, split_axis=0, concat_axis=0, tiled=True)
    return blocks.reshape(rows.shape)


def on_device(tokens, expert_ids, gate_quanta, w_gate, w_up, w_down):
    experts = lax.axis_size("node") * lax.axis_size("local")
    capacity = tokens.shape[0] * expert_ids.shape[1] * 9 // 8
    ids_t = expert_ids.T
    weights = (w_gate[0], w_up[0], w_down[0])
    out_a, ranks = dispatch_a(ids_t, tokens, experts)
    in_a = exchange(out_a)
    out_b = dispatch_b(ranks, tokens)
    in_a, out_b = lax.optimization_barrier((in_a, out_b))
    in_b = exchange(out_b)
    done_a = expert(PARTS_A, in_a, in_a, *weights, capacity, "expert_a")
    back_a = exchange(done_a)
    done_b = expert(PARTS_B, in_b, in_a, *weights, capacity, "expert_b")
    back_a, done_b = lax.optimization_barrier((back_a, done_b))
    back_b = exchange(done_b)
    partial, weight = combine_a(ids_t, gate_quanta.T, ranks, back_a, tokens.shape[1])
    return combine_b(partial, weight, back_b)


def solution(mesh):
    rows = P(AXES, None)
    weights = P(AXES, None, None)
    return jax.shard_map(
        on_device,
        mesh=mesh,
        in_specs=(rows, rows, rows, weights, weights, weights),
        out_specs=rows,
        check_vma=False,
    )
```
